256 devices in a mesh: dom: 32 (over z, y), member: 8 (over x, core).
Axes of the slice: x: 4, y: 4, z: 8, core: 2. Of those that a mesh axis runs over, the one named last changes fastest.
Arguments:
- state: float32 [64, 3072, 512], P('member', 'dom'), may hold values from -6 to 6
- noise: bfloat16 [8, 64, 3072, 512], P(None, 'member', 'dom'), may hold values from -1.75 to 1.75
- w_local: bfloat16 [512, 512], replicated, may hold values from -0.25 to 0.25
- conn_weight: float32 [16, 3072], P(None, 'dom'), may hold values from -1.75 to 1.75
- conn_index: int32 [16, 3072], P(None, 'dom'), may hold values from 0 to 223, as said below
- boundary: int32 [32, 8], P('dom'), may hold values from 0 to 95, as said below
- send_pos: int32 [32, 32, 4], replicated, may hold values from 0 to 7
- readout: float32 [512], replicated, may hold values from -0.25 to 0.25
- observed: int32 [32, 64], P('dom'), may hold values from 0 to 95, as said below
- obs_value: float32 [32, 64], P('dom'), may hold values from -6 to 6
- obs_var: float32 [32, 64], P('dom'), may hold values from 0.1 to 1
- obs_pert: float32 [64, 32, 64], P('member', 'dom'), may hold values from -6 to 6
Outputs:
- analysis: float32 [64, 3072, 512], P('member', 'dom')
The draws below stay inside these ranges and needn't reach their ends.
Inputs may be any that keep to these rules, and one draw needn't show every extreme that they name: `conn_index`: each voxel's inputs number 12 rows of its own part (below 96) and 4 received slots; every slot is read by some voxel of its part. Each part's boundary rows are distinct. Each part's observed rows are distinct.
All inputs are finite; a program needn't handle non-finite values.
Results may differ from the reference program's by a relative error of at most 0.025.
Values may be sent and summed in bfloat16 or wider, within the bound.
No kernel may reach another device: no remote copies, remote signals or barrier semaphores. Data moves between devices by JAX's collectives and lax.ppermute only.
A program may use at most 64 MiB of HBM per device.

```python
import math
import jax
import jax.numpy as jnp
from jax import lax

STATE = 512
VOX_DEV = 96
STEPS = 8
CAP = 4
BND = 8
OBS = 64
KL = 12
KH = 4
KIN = 16
HALO = 128
VOXELS = 3072
MEMBERS = 64
N_DOM = 32


def part_perms(key, length):
    keys = jax.random.split(key, N_DOM)
    return jax.vmap(lambda single: jax.random.permutation(single, length))(keys).astype(jnp.int32)


def draw_conn_index(key, part):
    local_rows = jax.random.randint(jax.random.fold_in(key, 11), (KL, VOXELS), 0, VOX_DEV).astype(jnp.int32)
    perms = part_perms(jax.random.fold_in(key, 12), HALO)
    position = (jnp.arange(VOX_DEV, dtype=jnp.int32)[None, :] * KH + jnp.arange(KH, dtype=jnp.int32)[:, None]) % HALO
    halo_rows = perms[:, position]
    halo_rows = jnp.transpose(halo_rows, (1, 0, 2)).reshape(KH, VOXELS) + VOX_DEV
    return jnp.concatenate([local_rows, halo_rows.astype(jnp.int32)], axis=0)


def draw_boundary(key, part):
    return part_perms(jax.random.fold_in(key, 21), VOX_DEV)[:, :BND]


def draw_observed(key, part):
    return part_perms(jax.random.fold_in(key, 31), VOX_DEV)[:, :OBS]


def place_ends(result, own_key, low, largest):
    extent = result.shape
    place = [jax.random.randint(jax.random.fold_in(own_key, axis), (), 0, extent[axis]) for axis in range(len(extent))]
    result = result.at[tuple(place)].set(low)
    longest = extent.index(max(extent))
    place[longest] = (place[longest] + 1) % extent[longest]
    return result.at[tuple(place)].set(largest)


def shard_levels(key, extent, cuts, least, high):
    level = 1.0
    for dim, blocks in cuts:
        steps = jax.random.uniform(jax.random.fold_in(jax.random.fold_in(key, 6), dim), (blocks,), jnp.float32, least / len(cuts), high / len(cuts))
        level = level * jnp.repeat(jnp.exp(steps), extent[dim] // blocks).reshape((-1,) + (1,) * (len(extent) - 1 - dim))
    return level


def centred(key, extent, width, limit, cuts=(), kind=jnp.bfloat16):
    values = jax.random.normal(key, extent, jnp.float32) * width
    if len(cuts) > 0:
        values = shard_levels(key, extent, cuts, -0.22, 0.18) * values
    return jnp.clip(values, min=-limit, max=limit).astype(kind)


def setup_inputs(seed: int = 0) -> dict:
    seeds = jax.random.split(jax.random.key(seed), 13)
    state = centred(seeds[0], (MEMBERS, VOXELS, STATE), 1.0, 6.0, ((0, 8), (1, 32)), jnp.float32)
    noise = centred(seeds[1], (STEPS, MEMBERS, VOXELS, STATE), 0.3, 1.75, ((1, 8), (2, 32)))
    w_local = centred(seeds[2], (STATE, STATE), STATE ** -0.5, 0.25)
    conn_weight = centred(seeds[3], (KIN, VOXELS), 0.3, 1.75, ((1, 32),), jnp.float32)
    conn_index = draw_conn_index(jax.random.fold_in(seeds[12], 71), 0)
    boundary = draw_boundary(jax.random.fold_in(seeds[12], 71), 0)
    send_pos = place_ends(jax.random.randint(seeds[6], (N_DOM, N_DOM, CAP), 0, BND), jax.random.fold_in(seeds[6], 1), 0, BND - 1).astype(jnp.int32)
    readout = centred(seeds[7], (STATE,), 0.044, 0.25, (), jnp.float32)
    observed = draw_observed(jax.random.fold_in(seeds[12], 71), 0)
    obs_value = centred(seeds[9], (N_DOM, OBS), 1.0, 6.0, ((0, 32),), jnp.float32)
    obs_var = jnp.clip(jnp.exp(math.log(1.0) - 2.3025851 * jax.random.uniform(seeds[10], (N_DOM, OBS), jnp.float32) ** shard_levels(seeds[10], (N_DOM, OBS), ((0, 32),), -0.2, 0.2)), 0.1, 1.0)
    obs_pert = centred(seeds[11], (MEMBERS, N_DOM, OBS), 1.0, 6.0, ((0, 8), (1, 32)), jnp.float32)
    return dict(state=state, noise=noise, w_local=w_local, conn_weight=conn_weight, conn_index=conn_index, boundary=boundary, send_pos=send_pos, readout=readout, observed=observed, obs_value=obs_value, obs_var=obs_var, obs_pert=obs_pert)


RELAX_RATE = 0.5

def mixing_matrix(image_part, innov_part, var_part):
    members_count = image_part.shape[0]
    anomaly = image_part - lax.optimization_barrier(jnp.mean(image_part, axis=0, keepdims=True))
    covar = jnp.dot(anomaly.T, anomaly, precision=lax.Precision.HIGHEST) / (members_count - 1) + jnp.diag(var_part)
    gain = jnp.linalg.solve(covar, innov_part.T).T
    mixing = jnp.dot(gain, anomaly.T, precision=lax.Precision.HIGHEST) / (members_count - 1)
    return mixing - lax.optimization_barrier(jnp.mean(mixing, axis=1, keepdims=True))

def reference(state, noise, w_local, conn_weight, conn_index, boundary, send_pos, readout, observed, obs_value, obs_var, obs_pert):
    parts = jnp.arange(N_DOM, dtype=jnp.int32)
    flipped = jnp.transpose(send_pos, (1, 0, 2))
    slot_rows = parts[None, :, None] * VOX_DEV + boundary[parts[None, :, None], flipped]
    slot_rows = slot_rows.reshape(N_DOM, HALO).astype(jnp.int32)
    part_of = jnp.arange(VOXELS, dtype=jnp.int32) // VOX_DEV
    halo_pos = jnp.clip(conn_index - VOX_DEV, 0, HALO - 1)
    global_index = jnp.where(conn_index < VOX_DEV, part_of[None, :] * VOX_DEV + conn_index, slot_rows[part_of[None, :], halo_pos]).astype(jnp.int32)
    current = state
    for step_index in range(STEPS):
        rate = jnp.tanh(current).astype(jnp.bfloat16)

        def add_input(which, total):
            picked = jnp.take(rate, global_index[which], axis=1).astype(jnp.float32)
            return total + conn_weight[which][None, :, None] * picked
        drive = lax.fori_loop(0, KIN, add_input, jnp.zeros(current.shape, jnp.float32))
        inputs = (rate.astype(jnp.float32) + drive).astype(jnp.bfloat16)
        mixed = jnp.dot(inputs.reshape(-1, STATE).astype(jnp.float32), w_local.astype(jnp.float32), preferred_element_type=jnp.float32).reshape(current.shape)
        current = (1.0 - RELAX_RATE) * current + RELAX_RATE * mixed + noise[step_index].astype(jnp.float32)
    rows_observed = (parts[:, None] * VOX_DEV + observed).reshape(-1).astype(jnp.int32)
    picked_obs = jnp.take(current, rows_observed, axis=1)
    image = jnp.einsum('mos,s->mo', picked_obs, readout, precision=lax.Precision.HIGHEST).reshape(MEMBERS, N_DOM, OBS)
    innov = obs_value[None] + jnp.sqrt(obs_var)[None] * obs_pert - image
    mixing = jax.vmap(mixing_matrix, in_axes=(1, 1, 0))(image, innov, obs_var)
    blocks = current.reshape(MEMBERS, N_DOM, VOX_DEV * STATE)
    update = jnp.einsum('pmj,jpf->mpf', mixing, blocks, precision=lax.Precision.HIGHEST)
    return (blocks + update).reshape(MEMBERS, VOXELS, STATE)
```

```python
import functools

import jax
import jax.numpy as jnp
from jax import lax
from jax.experimental import pallas as pl
from jax.experimental.pallas import tpu as pltpu
from jax.sharding import Mesh, PartitionSpec as P

STATE = 512
VOX = 96
STEPS = 8
BND = 8
OBS = 64
KIN = 16
HALO = 128
PARTS = 8
RING = 4
ROWS = PARTS * BND
AUX = 16
TAIL = 8
CHUNK = 48
MEMBERS = 64
BF = jnp.bfloat16
F32 = jnp.float32
HIGH = lax.Precision.HIGHEST


def iota(shape, axis):
    return lax.broadcasted_iota(jnp.int32, shape, axis)


def dot(a, b):
    return jnp.dot(a, b, preferred_element_type=F32)


def pieces(value):
    high = value.astype(BF).astype(F32)
    rest = value - high
    middle = rest.astype(BF).astype(F32)
    return high, middle, rest - middle


def stack_rows(rows, shape):
    row = iota(shape, 0)
    total = jnp.zeros(shape, F32)
    for place, value in enumerate(rows):
        total = jnp.where(row == place, jnp.broadcast_to(value, shape), total)
    return total


def chosen_rows(bound):
    eye = iota((AUX, BND), 0) == iota((AUX, BND), 1)
    column = jnp.sum(jnp.where(eye, bound.astype(F32), 0.0), axis=1, keepdims=True)
    shape = (AUX, 128)
    match = (iota(shape, 1).astype(F32) == column) & (iota(shape, 0) < BND)
    return jnp.where(match, 1.0, 0.0).astype(BF)


def prep_body(state, weight, index, bound, observed, value, var, pert, slab):
    chosen = chosen_rows(bound[...])
    for j in range(2):
        rate = jnp.tanh(state[j]).astype(BF)
        slab[j, 0:VOX, :] = rate
        slab[j, VOX : VOX + AUX, :] = jnp.zeros((AUX, STATE), BF)
        slab[j, VOX : VOX + AUX, 0:VOX] = weight[...].astype(BF)
        slab[j, VOX : VOX + AUX, 128 : 128 + VOX] = index[...].astype(F32).astype(BF)
        shifted = value[...] + jnp.sqrt(var[...]) * pert[j]
        info = (observed[...].astype(F32),) + pieces(shifted)
        slab[j, VOX : VOX + AUX, 256 : 256 + OBS] = stack_rows(info, (AUX, OBS)).astype(BF)
        slab[j, VOX : VOX + AUX, 384:512] = chosen
        slab[j, VOX + AUX : VOX + AUX + BND, :] = dot(chosen[:, 0:VOX], rate)[0:BND].astype(BF)


SMALL = pltpu.CompilerParams(vmem_limit_bytes=20 * 2**20)


def whole(*shape):
    return pl.BlockSpec(shape, lambda q: (0,) * len(shape))


def prep(state, weight, index, bound, observed, value, var, pert):
    return pl.pallas_call(
        prep_body,
        grid=(PARTS // 2,),
        in_specs=[
            pl.BlockSpec((2, VOX, STATE), lambda j: (j, 0, 0)),
            whole(KIN, VOX),
            whole(KIN, VOX),
            whole(1, BND),
            whole(1, OBS),
            whole(1, OBS),
            whole(1, OBS),
            pl.BlockSpec((2, 1, OBS), lambda j: (j, 0, 0)),
        ],
        out_specs=pl.BlockSpec((2, VOX + AUX + BND, STATE), lambda j: (j, 0, 0)),
        out_shape=jax.ShapeDtypeStruct((PARTS, VOX + AUX + BND, STATE), BF),
        name="prep",
        compiler_params=SMALL,
    )(state, weight, index, bound, observed, value, var, pert)


def pack_body(state, noise, bound, first, *packed):
    chosen = chosen_rows(bound[...])[:, 0:VOX]
    start = (0.5 * state[0] + noise[0, 0].astype(F32)).astype(BF)
    first[0, 0:VOX, :] = start
    for t in range(STEPS):
        rows = start if t == 0 else noise[t, 0]
        first[0, VOX + t * BND : VOX + (t + 1) * BND, :] = dot(chosen, rows)[0:BND].astype(BF)
    for steps, out in zip(BATCHES, packed):
        for place, t in enumerate(steps):
            out[0, place] = noise[t, 0]


BATCHES = ((1,), (2, 3), (4, 5), (6, 7))


def pack(state, noise, bound):
    sizes = [len(steps) for steps in BATCHES]
    return pl.pallas_call(
        pack_body,
        grid=(PARTS,),
        in_specs=[
            pl.BlockSpec((1, VOX, STATE), lambda j: (j, 0, 0)),
            pl.BlockSpec((STEPS, 1, VOX, STATE), lambda j: (0, j, 0, 0)),
            whole(1, BND),
        ],
        out_specs=[pl.BlockSpec((1, VOX + STEPS * BND, STATE), lambda j: (j, 0, 0))]
        + [pl.BlockSpec((1, n, VOX, STATE), lambda j: (j, 0, 0, 0)) for n in sizes],
        out_shape=[jax.ShapeDtypeStruct((PARTS, VOX + STEPS * BND, STATE), BF)]
        + [jax.ShapeDtypeStruct((PARTS, n, VOX, STATE), BF) for n in sizes],
        name="pack",
        compiler_params=SMALL,
        cost_estimate=pl.CostEstimate(flops=10**9, bytes_accessed=14 * 10**6, transcendentals=0),
    )(state, noise, bound)


def tables_body(slab, colmap, own, halo, pick, ahead, start):
    weight = slab[0, VOX : VOX + AUX, 0:128].astype(F32)
    index = slab[0, VOX : VOX + AUX, 128:256].astype(F32)
    row = iota((256, 128), 0).astype(F32)
    spread = jnp.zeros((256, 128), F32)
    for k in range(KIN):
        spread = spread + jnp.where(row == index[k : k + 1, :], weight[k : k + 1, :], 0.0)
    local = jnp.transpose(spread[0:128, :])[0:VOX, :]
    slots = jnp.transpose(spread[VOX : VOX + HALO, :])[0:VOX, :].astype(BF)
    place = (iota((RING * ROWS, HALO), 0) == colmap[0]).astype(F32).astype(BF)
    far = lax.dot_general(slots, place, (((1,), (1,)), ((), ())), preferred_element_type=F32).astype(BF)
    chosen = slab[0, VOX : VOX + AUX, 384:512][:, 0:VOX]
    own_matrix = local[:, 0:VOX].astype(BF)
    own[0] = own_matrix
    halo[0] = far
    chosen_own = dot(chosen, own_matrix)
    both = jnp.concatenate([chosen.astype(F32)[0:BND], chosen_own[0:BND]], axis=0).astype(BF)
    pick[0] = both
    ahead[...] = dot(chosen, far)[0:BND].astype(BF)
    found = dot(both, slab[0, 0:VOX, :])
    start[...] = found[0:BND] + found[BND : 2 * BND]


def tables(slab, colmap):
    return pl.pallas_call(
        tables_body,
        grid=(PARTS,),
        in_specs=[
            pl.BlockSpec((1, VOX + AUX, STATE), lambda q: (q, 0, 0)),
            pl.BlockSpec((1, 1, HALO), lambda q: (q, 0, 0)),
        ],
        out_specs=[
            pl.BlockSpec((1, VOX, VOX), lambda q: (q, 0, 0)),
            pl.BlockSpec((1, VOX, RING * ROWS), lambda q: (q, 0, 0)),
            pl.BlockSpec((1, 2 * BND, VOX), lambda q: (q, 0, 0)),
            pl.BlockSpec((BND, RING * ROWS), lambda q: (q, 0)),
            pl.BlockSpec((BND, STATE), lambda q: (q, 0)),
        ],
        out_shape=[
            jax.ShapeDtypeStruct((PARTS, VOX, VOX), BF),
            jax.ShapeDtypeStruct((PARTS, VOX, RING * ROWS), BF),
            jax.ShapeDtypeStruct((PARTS, 2 * BND, VOX), BF),
            jax.ShapeDtypeStruct((ROWS, RING * ROWS), BF),
            jax.ShapeDtypeStruct((ROWS, STATE), F32),
        ],
        name="tables",
        compiler_params=SMALL,
        cost_estimate=pl.CostEstimate(flops=10**9, bytes_accessed=10**7, transcendentals=0),
    )(slab, colmap)


def edge_body(begin, ahead, w, noise, r0, r1, r2, r3, *refs):
    current, (rate_out, current_out) = refs[:-2], refs[-2:]
    table = jnp.concatenate([r0[...], r1[...], r2[...], r3[...]], axis=0)
    inputs = (begin[...] + dot(ahead[...], table)).astype(BF)
    value = 0.5 * dot(inputs, w[...]) + noise[...].astype(F32).reshape(ROWS, STATE)
    if current:
        value = value + 0.5 * current[0][...]
    current_out[...] = value
    rate_out[...] = jnp.tanh(value).astype(BF)


def edge(t, begin, ahead, w, first, table, current):
    more = [] if current is None else [current]
    return pl.pallas_call(
        edge_body,
        grid=(1,),
        in_specs=[
            whole(ROWS, STATE),
            whole(ROWS, RING * ROWS),
            whole(STATE, STATE),
            pl.BlockSpec((PARTS, BND, STATE), lambda q: (0, VOX // BND + t, 0)),
        ]
        + [whole(ROWS, STATE)] * (RING + len(more)),
        out_specs=[whole(ROWS, STATE), whole(ROWS, STATE)],
        out_shape=[
            jax.ShapeDtypeStruct((ROWS, STATE), BF),
            jax.ShapeDtypeStruct((ROWS, STATE), F32),
        ],
        name="edge",
        compiler_params=SMALL,
        cost_estimate=pl.CostEstimate(flops=10**8, bytes_accessed=10**6, transcendentals=0),
    )(begin, ahead, w, first, *table, *more)


GROUP = 4


def advance(rate, own, halo, w, noise, current, table):
    mine = jnp.concatenate([dot(own[i], rate[i]) for i in range(GROUP)], axis=0)
    matrix = jnp.concatenate([halo[i] for i in range(GROUP)], axis=0)
    far = dot(matrix, jnp.concatenate([r[...] for r in table], axis=0))
    inputs = rate[...].astype(F32).reshape(GROUP * VOX, STATE) + mine + far
    mixed = dot(inputs.astype(BF), w[...])
    value = 0.5 * mixed + noise[...].astype(F32).reshape(GROUP * VOX, STATE)
    if current is not None:
        value = value + 0.5 * current[...].reshape(GROUP * VOX, STATE)
    return value


def step_body(has_current, *refs):
    rate, own, halo, pick, w, noise = refs[:6]
    refs = refs[6:]
    current = None
    if has_current:
        current, refs = refs[0], refs[1:]
    table, (current_out, rate_out, begin_out) = refs[:RING], refs[RING:]
    value = advance(rate, own, halo, w, noise, current, table)
    fresh = jnp.tanh(value).astype(BF)
    current_out[...] = value.reshape(GROUP, VOX, STATE)
    rate_out[...] = fresh.reshape(GROUP, VOX, STATE)
    for i in range(GROUP):
        found = dot(pick[i], fresh[i * VOX : (i + 1) * VOX])
        begin_out[i * BND : (i + 1) * BND, :] = found[0:BND] + found[BND : 2 * BND]


def common_specs(has_current, with_pick, place):
    part = lambda *shape: pl.BlockSpec((GROUP,) + shape, lambda q: (q, 0, 0))
    kick = part(VOX, STATE)
    if place is not None:
        kick = pl.BlockSpec((GROUP, 1, VOX, STATE), lambda q: (q, place, 0, 0))
    specs = [part(VOX, STATE), part(VOX, VOX), part(VOX, RING * ROWS)]
    if with_pick:
        specs.append(part(2 * BND, VOX))
    specs += [whole(STATE, STATE), kick]
    if has_current:
        specs.append(part(VOX, STATE))
    specs += [whole(ROWS, STATE)] * RING
    return specs


STEP_COST = pl.CostEstimate(flops=2 * 10**9, bytes_accessed=6 * 10**6, transcendentals=4 * 10**5)


def step(rate, own, halo, pick, w, noise, place, current, table):
    args = [rate, own, halo, pick, w, noise] + ([] if current is None else [current]) + list(table)
    return pl.pallas_call(
        functools.partial(step_body, current is not None),
        grid=(PARTS // GROUP,),
        in_specs=common_specs(current is not None, True, place),
        out_specs=[
            pl.BlockSpec((GROUP, VOX, STATE), lambda q: (q, 0, 0)),
            pl.BlockSpec((GROUP, VOX, STATE), lambda q: (q, 0, 0)),
            pl.BlockSpec((GROUP * BND, STATE), lambda q: (q, 0)),
        ],
        out_shape=[
            jax.ShapeDtypeStruct((PARTS, VOX, STATE), F32),
            jax.ShapeDtypeStruct((PARTS, VOX, STATE), BF),
            jax.ShapeDtypeStruct((ROWS, STATE), F32),
        ],
        name="step",
        compiler_params=SMALL,
        cost_estimate=STEP_COST,
    )(*args)


def last_body(rate, own, halo, w, noise, current, r0, r1, r2, r3, extra, readout, out):
    value = advance(rate, own, halo, w, noise, current, (r0, r1, r2, r3))
    weighted = value * readout[...]
    for i in range(GROUP):
        image_rows = jnp.sum(weighted[i * VOX : (i + 1) * VOX], axis=1, keepdims=True)
        info = extra[i].astype(F32)
        observed = info[0:1, 0:OBS]
        shifted = info[1:2, 0:OBS] + info[2:3, 0:OBS] + info[3:4, 0:OBS]
        seen = iota((VOX, OBS), 0).astype(F32) == observed
        image = jnp.sum(jnp.where(seen, image_rows, 0.0), axis=0, keepdims=True)
        image_block = stack_rows(pieces(image), (TAIL, OBS)).astype(BF)
        innov_block = stack_rows(pieces(shifted - image), (TAIL, OBS)).astype(BF)
        for c in range(8):
            high, quarter = divmod(c, 4)
            begin = i * VOX + high * CHUNK
            out[i * 8 + c, 0:CHUNK, :] = value[
                begin : begin + CHUNK, quarter * 128 : (quarter + 1) * 128
            ].astype(BF)
            out[i * 8 + c, CHUNK : CHUNK + TAIL, 0:OBS] = image_block
            out[i * 8 + c, CHUNK : CHUNK + TAIL, OBS : 2 * OBS] = innov_block


def last(rate, own, halo, w, noise, place, current, table, slab, readout):
    return pl.pallas_call(
        last_body,
        grid=(PARTS // GROUP,),
        in_specs=common_specs(True, False, place)
        + [
            pl.BlockSpec((GROUP, AUX, 128), lambda q: (q, VOX // AUX, 2)),
            pl.BlockSpec((1, STATE), lambda q: (0, 0)),
        ],
        out_specs=pl.BlockSpec((GROUP * 8, CHUNK + TAIL, 128), lambda q: (q, 0, 0)),
        out_shape=jax.ShapeDtypeStruct((PARTS * 8, CHUNK + TAIL, 128), BF),
        name="last",
        compiler_params=SMALL,
        cost_estimate=STEP_COST,
    )(rate, own, halo, w, noise, current, *table, slab, readout)


def analyse_body(data, var, out):
    extra = data[:, CHUNK : CHUNK + TAIL, :].astype(F32)
    both = jnp.sum(extra, axis=1)
    image, innov = both[:, 0:OBS], both[:, OBS : 2 * OBS]
    anomaly = image - jnp.mean(image, axis=0, keepdims=True)
    flipped = jnp.transpose(anomaly)
    covar = jnp.dot(flipped, anomaly, precision=HIGH, preferred_element_type=F32) / (MEMBERS - 1)
    square = (OBS, OBS)
    covar = covar + jnp.where(iota(square, 0) == iota(square, 1), var[...], 0.0)
    work = jnp.concatenate([covar, flipped], axis=1)
    row = iota((OBS, 2 * OBS), 0)
    for k in range(OBS):
        pivot = work[k : k + 1, :] / work[k : k + 1, k : k + 1]
        work = jnp.where(row == k, pivot, work - work[:, k : k + 1] * pivot)
    solved = work[:, OBS : 2 * OBS]
    mixing = jnp.dot(innov, solved, precision=HIGH, preferred_element_type=F32) / (MEMBERS - 1)
    mixing = mixing - jnp.mean(mixing, axis=1, keepdims=True)
    wide = MEMBERS * 16
    repeat = jnp.where(
        lax.shift_right_logical(iota((wide, MEMBERS), 0), 4) == iota((wide, MEMBERS), 1), 1.0, 0.0
    ).astype(BF)
    tall = dot(repeat, mixing.astype(BF)).astype(BF)
    large = lax.dot_general(tall, repeat, (((1,), (1,)), ((), ())), preferred_element_type=F32)
    same = (iota((wide, wide), 0) & 15) == (iota((wide, wide), 1) & 15)
    large = jnp.where(same, large, 0.0).astype(BF)
    for b in range(CHUNK // 16):
        rows = data[:, b * 16 : (b + 1) * 16, :].reshape(wide, 128)
        result = (rows.astype(F32) + dot(large, rows)).astype(BF).reshape(MEMBERS, 16, 128)
        for m in range(MEMBERS):
            out[m % 8, m // 8, b * 16 : (b + 1) * 16, :] = result[m]


def analyse(data, var):
    return pl.pallas_call(
        analyse_body,
        out_shape=jax.ShapeDtypeStruct((8, 8, CHUNK, 128), BF),
        name="analyse",
        compiler_params=pltpu.CompilerParams(vmem_limit_bytes=32 * 2**20),
    )(data, var)


def finish_body(data, out):
    for j in range(4):
        for c in range(8):
            high, quarter = divmod(c, 4)
            out[j, high * CHUNK : (high + 1) * CHUNK, quarter * 128 : (quarter + 1) * 128] = data[
                c, j
            ].astype(F32)


def finish(data):
    return pl.pallas_call(
        finish_body,
        grid=(2,),
        in_specs=[pl.BlockSpec((8, 4, CHUNK, 128), lambda j: (0, j, 0, 0))],
        out_specs=pl.BlockSpec((4, VOX, STATE), lambda j: (j, 0, 0)),
        out_shape=jax.ShapeDtypeStruct((8, VOX, STATE), F32),
        name="finish",
        compiler_params=SMALL,
    )(data)


def swap(value, axes):
    return lax.all_to_all(value, axes, split_axis=0, concat_axis=0, tiled=True)


def per_device(
    state,
    noise,
    w_local,
    conn_weight,
    conn_index,
    boundary,
    send_pos,
    readout,
    observed,
    obs_value,
    obs_var,
    obs_pert,
):
    here = lax.axis_index("zh")
    group = ("zl", "y")
    slab = prep(
        state, conn_weight, conn_index, boundary, observed, obs_value, obs_var, obs_pert
    )
    slab = swap(slab, group)
    first, *packed = pack(state, noise, boundary)
    edge_rate = slab[:, VOX + AUX :, :].reshape(ROWS, STATE)
    sends = lax.dynamic_slice_in_dim(send_pos, here * PARTS, PARTS, 1)
    source = jnp.arange(RING * PARTS, dtype=jnp.int32)
    base = jnp.remainder(here - source // PARTS, RING) * ROWS + (source % PARTS) * BND
    colmap = jnp.transpose(base[:, None, None] + sends, (1, 0, 2)).reshape(PARTS, 1, HALO)
    own, halo, pick, ahead, begin = tables(slab, colmap)
    first = swap(first, group)
    kicks = {0: (first, None)}
    for steps, array in zip(BATCHES, packed):
        array = swap(array, group)
        for place, t in enumerate(steps):
            kicks[t] = (array, place)
    edge_current = current = None
    rate = slab
    for t in range(STEPS):
        table = [edge_rate]
        for o in range(1, RING):
            table.append(lax.ppermute(edge_rate, "zh", [(i, (i + o) % RING) for i in range(RING)]))
        kick, place = kicks[t]
        if t < STEPS - 1:
            edge_rate, edge_current = edge(t, begin, ahead, w_local, first, table, edge_current)
            current, rate, begin = step(
                rate, own, halo, pick, w_local, kick, place, current, table
            )
        else:
            chunks = last(
                rate, own, halo, w_local, kick, place, current, table, slab, readout[None, :]
            )
    gathered = swap(chunks, ("zl", "y", "x", "core"))
    result = swap(analyse(gathered, obs_var), ("x", "core"))
    return finish(result)


def solution(mesh):
    fine = Mesh(mesh.devices.reshape(RING, 2, 4, 4, 2), ("zh", "zl", "y", "x", "core"))
    dom, member = ("zh", "zl", "y"), ("x", "core")
    in_specs = (
        P(member, dom, None),
        P(None, member, dom, None),
        P(),
        P(None, dom),
        P(None, dom),
        P(dom, None),
        P(),
        P(),
        P(dom, None),
        P(dom, None),
        P(dom, None),
        P(member, dom, None),
    )
    return jax.shard_map(
        per_device, mesh=fine, in_specs=in_specs, out_specs=P(member, dom, None), check_vma=False
    )
```

```python
import functools

import jax
import jax.numpy as jnp
from jax import lax
from jax.experimental import pallas as pl
from jax.experimental.pallas import tpu as pltpu
from jax.sharding import Mesh, PartitionSpec as P

STATE = 512
VOX = 96
STEPS = 8
BND = 8
OBS = 64
KIN = 16
HALO = 128
PARTS = 8
RING = 4
DEPTH, WIDTH, LENGTH, CORES = 8, 4, 4, 2
ROWS = PARTS * BND
AUX = 16
TAIL = 8
CHUNK = 48
MEMBERS = 64
BF = jnp.bfloat16
F32 = jnp.float32
HIGH = lax.Precision.HIGHEST


def iota(shape, axis):
    return lax.broadcasted_iota(jnp.int32, shape, axis)


def dot(a, b):
    return jnp.dot(a, b, preferred_element_type=F32)


def pieces(value):
    high = value.astype(BF).astype(F32)
    rest = value - high
    middle = rest.astype(BF).astype(F32)
    return high, middle, rest - middle


def stack_rows(rows, shape):
    row = iota(shape, 0)
    total = jnp.zeros(shape, F32)
    for place, value in enumerate(rows):
        total = jnp.where(row == place, jnp.broadcast_to(value, shape), total)
    return total


def chosen_rows(bound):
    eye = iota((AUX, BND), 0) == iota((AUX, BND), 1)
    column = jnp.sum(jnp.where(eye, bound.astype(F32), 0.0), axis=1, keepdims=True)
    shape = (AUX, 128)
    match = (iota(shape, 1).astype(F32) == column) & (iota(shape, 0) < BND)
    return jnp.where(match, 1.0, 0.0).astype(BF)


def prep_body(state, noise, weight, index, bound, observed, value, var, pert, slab):
    chosen = chosen_rows(bound[...])
    for j in range(2):
        rate = jnp.tanh(state[j]).astype(BF)
        slab[j, 0:VOX, :] = rate
        slab[j, VOX : VOX + AUX, :] = jnp.zeros((AUX, STATE), BF)
        slab[j, VOX : VOX + AUX, 0:VOX] = weight[...].astype(BF)
        slab[j, VOX : VOX + AUX, 128 : 128 + VOX] = index[...].astype(F32).astype(BF)
        shifted = value[...] + jnp.sqrt(var[...]) * pert[j]
        info = (observed[...].astype(F32),) + pieces(shifted)
        slab[j, VOX : VOX + AUX, 256 : 256 + OBS] = stack_rows(info, (AUX, OBS)).astype(BF)
        slab[j, VOX : VOX + AUX, 384:512] = chosen
        start = (0.5 * state[j] + noise[0, j].astype(F32)).astype(BF)
        pick = chosen[:, 0:VOX]
        both = (dot(pick, rate)[0:BND], dot(pick, start)[0:BND])
        slab[j, VOX + AUX : VOX + 2 * AUX, :] = jnp.concatenate(both, axis=0).astype(BF)


ROOMY = tuple(range(8))
SMALL = pltpu.CompilerParams(vmem_limit_bytes=20 * 2**20)


def whole(*shape):
    return pl.BlockSpec(shape, lambda q: (0,) * len(shape))


def prep(state, noise, weight, index, bound, observed, value, var, pert):
    return pl.pallas_call(
        prep_body,
        grid=(PARTS // 2,),
        in_specs=[
            pl.BlockSpec((2, VOX, STATE), lambda j: (j, 0, 0)),
            pl.BlockSpec((1, 2, VOX, STATE), lambda j: (0, j, 0, 0)),
            whole(KIN, VOX),
            whole(KIN, VOX),
            whole(1, BND),
            whole(1, OBS),
            whole(1, OBS),
            whole(1, OBS),
            pl.BlockSpec((2, 1, OBS), lambda j: (j, 0, 0)),
        ],
        out_specs=pl.BlockSpec((2, VOX + 2 * AUX, STATE), lambda j: (j, 0, 0)),
        out_shape=jax.ShapeDtypeStruct((PARTS, VOX + 2 * AUX, STATE), BF),
        name="prep",
    )(state, noise, weight, index, bound, observed, value, var, pert)


def pack_body(state, noise, bound, first, *packed):
    chosen = chosen_rows(bound[...])[:, 0:VOX]
    start = (0.5 * state[0] + noise[0, 0].astype(F32)).astype(BF)
    first[0, 0:VOX, :] = start
    found = [dot(chosen, noise[t, 0])[0:BND].astype(BF) for t in range(1, STEPS)]
    found.append(jnp.zeros((BND, STATE), BF))
    first[0, VOX:, :] = found[0]
    for steps, out in zip(BATCHES, packed):
        for place, t in enumerate(steps):
            out[0, place, 0:VOX, :] = noise[t, 0]
            out[0, place, VOX:, :] = found[t]


BATCHES = ((1,), (2,), (3,), (4, 5), (6, 7))
FIRST = VOX + BND


def pack(state, noise, bound):
    sizes = [len(steps) for steps in BATCHES]
    return pl.pallas_call(
        pack_body,
        grid=(PARTS,),
        in_specs=[
            pl.BlockSpec((1, VOX, STATE), lambda j: (j, 0, 0)),
            pl.BlockSpec((STEPS, 1, VOX, STATE), lambda j: (0, j, 0, 0)),
            whole(1, BND),
        ],
        out_specs=[pl.BlockSpec((1, FIRST, STATE), lambda j: (j, 0, 0))]
        + [pl.BlockSpec((1, n, FIRST, STATE), lambda j: (j, 0, 0, 0)) for n in sizes],
        out_shape=[jax.ShapeDtypeStruct((PARTS, FIRST, STATE), BF)]
        + [jax.ShapeDtypeStruct((PARTS, n, FIRST, STATE), BF) for n in sizes],
        name="pack",
        cost_estimate=pl.CostEstimate(flops=10**9, bytes_accessed=14 * 10**6, transcendentals=0),
    )(state, noise, bound)


def tables_body(slab, colmap, own, halo, pick, ahead, start):
    weight = slab[0, VOX : VOX + AUX, 0:128].astype(F32)
    index = slab[0, VOX : VOX + AUX, 128:256].astype(F32)
    row = iota((256, 128), 0).astype(F32)
    spread = jnp.zeros((256, 128), F32)
    for k in range(KIN):
        spread = spread + jnp.where(row == index[k : k + 1, :], weight[k : k + 1, :], 0.0)
    local = jnp.transpose(spread[0:128, :])[0:VOX, :]
    slots = jnp.transpose(spread[VOX : VOX + HALO, :])[0:VOX, :].astype(BF)
    place = (iota((RING * ROWS, HALO), 0) == colmap[0]).astype(F32).astype(BF)
    far = lax.dot_general(slots, place, (((1,), (1,)), ((), ())), preferred_element_type=F32).astype(BF)
    chosen = slab[0, VOX : VOX + AUX, 384:512][:, 0:VOX]
    own_matrix = local[:, 0:VOX].astype(BF)
    own[0] = own_matrix
    halo[0] = far
    chosen_own = dot(chosen, own_matrix)
    both = jnp.concatenate([chosen.astype(F32)[0:BND], chosen_own[0:BND]], axis=0).astype(BF)
    pick[0] = both
    ahead[...] = dot(chosen, far)[0:BND].astype(BF)
    found = dot(both, slab[0, 0:VOX, :])
    start[...] = found[0:BND] + found[BND : 2 * BND]


def tables(slab, colmap):
    return pl.pallas_call(
        tables_body,
        grid=(PARTS,),
        in_specs=[
            pl.BlockSpec((1, VOX + AUX, STATE), lambda q: (q, 0, 0)),
            pl.BlockSpec((1, 1, HALO), lambda q: (q, 0, 0)),
        ],
        out_specs=[
            pl.BlockSpec((1, VOX, VOX), lambda q: (q, 0, 0)),
            pl.BlockSpec((1, VOX, RING * ROWS), lambda q: (q, 0, 0)),
            pl.BlockSpec((1, 2 * BND, VOX), lambda q: (q, 0, 0)),
            pl.BlockSpec((BND, RING * ROWS), lambda q: (q, 0)),
            pl.BlockSpec((BND, STATE), lambda q: (q, 0)),
        ],
        out_shape=[
            jax.ShapeDtypeStruct((PARTS, VOX, VOX), BF),
            jax.ShapeDtypeStruct((PARTS, VOX, RING * ROWS), BF),
            jax.ShapeDtypeStruct((PARTS, 2 * BND, VOX), BF),
            jax.ShapeDtypeStruct((ROWS, RING * ROWS), BF),
            jax.ShapeDtypeStruct((ROWS, STATE), F32),
        ],
        name="tables",
        compiler_params=SMALL,
        cost_estimate=pl.CostEstimate(flops=10**9, bytes_accessed=10**7, transcendentals=0),
    )(slab, colmap)


def edge_body(begin, ahead, w, noise, r0, r1, r2, r3, *refs):
    current, (rate_out, current_out) = refs[:-2], refs[-2:]
    table = jnp.concatenate([r0[...], r1[...], r2[...], r3[...]], axis=0)
    inputs = (begin[...] + dot(ahead[...], table)).astype(BF)
    value = 0.5 * dot(inputs, w[...]) + noise[...].astype(F32).reshape(ROWS, STATE)
    if current:
        value = value + 0.5 * current[0][...]
    current_out[...] = value
    rate_out[...] = jnp.tanh(value).astype(BF)


def edge(begin, ahead, w, noise, place, table, current):
    more = [] if current is None else [current]
    kind, place = place
    if kind == "rows":
        early = pl.BlockSpec((PARTS, BND, STATE), lambda q: (0, place, 0))
    else:
        early = pl.BlockSpec((PARTS, 1, BND, STATE), lambda q: (0, place, VOX // BND, 0))
    return pl.pallas_call(
        edge_body,
        grid=(1,),
        in_specs=[
            whole(ROWS, STATE),
            whole(ROWS, RING * ROWS),
            whole(STATE, STATE),
            early,
        ]
        + [whole(ROWS, STATE)] * (RING + len(more)),
        out_specs=[whole(ROWS, STATE), whole(ROWS, STATE)],
        out_shape=[
            jax.ShapeDtypeStruct((ROWS, STATE), BF),
            jax.ShapeDtypeStruct((ROWS, STATE), F32),
        ],
        name="edge",
        compiler_params=SMALL,
        cost_estimate=pl.CostEstimate(flops=10**8, bytes_accessed=10**6, transcendentals=0),
    )(begin, ahead, w, noise, *table, *more)


GROUP = 4


def advance(rate, own, halo, w, noise, current, table):
    mine = jnp.concatenate([dot(own[i], rate[i]) for i in range(GROUP)], axis=0)
    matrix = jnp.concatenate([halo[i] for i in range(GROUP)], axis=0)
    far = dot(matrix, jnp.concatenate([r[...] for r in table], axis=0))
    inputs = rate[...].astype(F32).reshape(GROUP * VOX, STATE) + mine + far
    mixed = dot(inputs.astype(BF), w[...])
    value = 0.5 * mixed + noise[...].astype(F32).reshape(GROUP * VOX, STATE)
    if current is not None:
        value = value + 0.5 * current[...].reshape(GROUP * VOX, STATE)
    return value


def step_body(has_current, *refs):
    rate, own, halo, pick, w, noise = refs[:6]
    refs = refs[6:]
    current = None
    if has_current:
        current, refs = refs[0], refs[1:]
    table, (current_out, rate_out, begin_out) = refs[:RING], refs[RING:]
    value = advance(rate, own, halo, w, noise, current, table)
    fresh = jnp.tanh(value).astype(BF)
    current_out[...] = value.reshape(GROUP, VOX, STATE)
    rate_out[...] = fresh.reshape(GROUP, VOX, STATE)
    for i in range(GROUP):
        found = dot(pick[i], fresh[i * VOX : (i + 1) * VOX])
        begin_out[i * BND : (i + 1) * BND, :] = found[0:BND] + found[BND : 2 * BND]


def common_specs(has_current, with_pick, place):
    part = lambda *shape: pl.BlockSpec((GROUP,) + shape, lambda q: (q, 0, 0))
    kind, place = place
    if kind == "rows":
        kick = pl.BlockSpec((GROUP, VOX, STATE), lambda q: (q, place, 0))
    else:
        kick = pl.BlockSpec((GROUP, 1, VOX, STATE), lambda q: (q, place, 0, 0))
    specs = [part(VOX, STATE), part(VOX, VOX), part(VOX, RING * ROWS)]
    if with_pick:
        specs.append(part(2 * BND, VOX))
    specs += [whole(STATE, STATE), kick]
    if has_current:
        specs.append(part(VOX, STATE))
    specs += [whole(ROWS, STATE)] * RING
    return specs


STEP_COST = pl.CostEstimate(flops=2 * 10**9, bytes_accessed=6 * 10**6, transcendentals=4 * 10**5)


def step(roomy, rate, own, halo, pick, w, noise, place, current, table):
    args = [rate, own, halo, pick, w, noise] + ([] if current is None else [current]) + list(table)
    return pl.pallas_call(
        functools.partial(step_body, current is not None),
        grid=(PARTS // GROUP,),
        in_specs=common_specs(current is not None, True, place),
        out_specs=[
            pl.BlockSpec((GROUP, VOX, STATE), lambda q: (q, 0, 0)),
            pl.BlockSpec((GROUP, VOX, STATE), lambda q: (q, 0, 0)),
            pl.BlockSpec((GROUP * BND, STATE), lambda q: (q, 0)),
        ],
        out_shape=[
            jax.ShapeDtypeStruct((PARTS, VOX, STATE), F32),
            jax.ShapeDtypeStruct((PARTS, VOX, STATE), BF),
            jax.ShapeDtypeStruct((ROWS, STATE), F32),
        ],
        name="step",
        compiler_params=None if roomy else SMALL,
        cost_estimate=STEP_COST,
    )(*args)


def last_body(rate, own, halo, w, noise, current, r0, r1, r2, r3, extra, readout, out):
    value = advance(rate, own, halo, w, noise, current, (r0, r1, r2, r3))
    weighted = value * readout[...]
    for i in range(GROUP):
        image_rows = jnp.sum(weighted[i * VOX : (i + 1) * VOX], axis=1, keepdims=True)
        info = extra[i].astype(F32)
        observed = info[0:1, 0:OBS]
        shifted = info[1:2, 0:OBS] + info[2:3, 0:OBS] + info[3:4, 0:OBS]
        seen = iota((VOX, OBS), 0).astype(F32) == observed
        image = jnp.sum(jnp.where(seen, image_rows, 0.0), axis=0, keepdims=True)
        image_block = stack_rows(pieces(image), (TAIL, OBS)).astype(BF)
        innov_block = stack_rows(pieces(shifted - image), (TAIL, OBS)).astype(BF)
        for c in range(8):
            high, quarter = divmod(c, 4)
            begin = i * VOX + high * CHUNK
            out[i * 8 + c, 0:CHUNK, :] = value[
                begin : begin + CHUNK, quarter * 128 : (quarter + 1) * 128
            ].astype(BF)
            out[i * 8 + c, CHUNK : CHUNK + TAIL, 0:OBS] = image_block
            out[i * 8 + c, CHUNK : CHUNK + TAIL, OBS : 2 * OBS] = innov_block


def last(rate, own, halo, w, noise, place, current, table, slab, readout):
    return pl.pallas_call(
        last_body,
        grid=(PARTS // GROUP,),
        in_specs=common_specs(True, False, place)
        + [
            pl.BlockSpec((GROUP, AUX, 128), lambda q: (q, VOX // AUX, 2)),
            pl.BlockSpec((1, STATE), lambda q: (0, 0)),
        ],
        out_specs=pl.BlockSpec((GROUP * 8, CHUNK + TAIL, 128), lambda q: (q, 0, 0)),
        out_shape=jax.ShapeDtypeStruct((PARTS * 8, CHUNK + TAIL, 128), BF),
        name="last",
        compiler_params=SMALL,
        cost_estimate=STEP_COST,
    )(rate, own, halo, w, noise, current, *table, slab, readout)


def analyse_body(core, kept, other, var, out, data):
    half = MEMBERS // 2
    is_first = core[0] == 0
    data[0:half] = jnp.where(is_first, kept[...], other[...])
    data[half:] = jnp.where(is_first, other[...], kept[...])
    extra = data[:, CHUNK : CHUNK + TAIL, :].astype(F32)
    both = jnp.sum(extra, axis=1)
    image, innov = both[:, 0:OBS], both[:, OBS : 2 * OBS]
    anomaly = image - jnp.mean(image, axis=0, keepdims=True)
    flipped = jnp.transpose(anomaly)
    covar = jnp.dot(flipped, anomaly, precision=HIGH, preferred_element_type=F32) / (MEMBERS - 1)
    square = (OBS, OBS)
    covar = covar + jnp.where(iota(square, 0) == iota(square, 1), var[...], 0.0)
    work = jnp.concatenate([covar, flipped], axis=1)
    row = iota((OBS, 2 * OBS), 0)
    for k in range(0, OBS, 2):
        upper, lower = work[k : k + 1, :], work[k + 1 : k + 2, :]
        a, b = upper[:, k : k + 1], upper[:, k + 1 : k + 2]
        c, d = lower[:, k : k + 1], lower[:, k + 1 : k + 2]
        scale = 1.0 / (a * d - b * c)
        one = (d * upper - b * lower) * scale
        two = (a * lower - c * upper) * scale
        rest = work - work[:, k : k + 1] * one - work[:, k + 1 : k + 2] * two
        work = jnp.where(row == k, one, jnp.where(row == k + 1, two, rest))
    solved = work[:, OBS : 2 * OBS]
    mixing = jnp.dot(innov, solved, precision=HIGH, preferred_element_type=F32) / (MEMBERS - 1)
    mixing = mixing - jnp.mean(mixing, axis=1, keepdims=True)
    wide = MEMBERS * 16
    repeat = jnp.where(
        lax.shift_right_logical(iota((wide, MEMBERS), 0), 4) == iota((wide, MEMBERS), 1), 1.0, 0.0
    ).astype(BF)
    tall = dot(repeat, mixing.astype(BF)).astype(BF)
    large = lax.dot_general(tall, repeat, (((1,), (1,)), ((), ())), preferred_element_type=F32)
    same = (iota((wide, wide), 0) & 15) == (iota((wide, wide), 1) & 15)
    large = jnp.where(same, large, 0.0).astype(BF)
    for b in range(CHUNK // 16):
        rows = data[:, b * 16 : (b + 1) * 16, :].reshape(wide, 128)
        result = (rows.astype(F32) + dot(large, rows)).astype(BF).reshape(MEMBERS, 16, 128)
        for m in range(MEMBERS):
            owner = (m % LENGTH) * CORES + m // half
            out[owner, m % half // LENGTH, b * 16 : (b + 1) * 16, :] = result[m]


def analyse(core, kept, other, var):
    vmem = pl.BlockSpec(memory_space=pltpu.VMEM)
    return pl.pallas_call(
        analyse_body,
        in_specs=[pl.BlockSpec(memory_space=pltpu.SMEM), vmem, vmem, vmem],
        out_specs=vmem,
        scratch_shapes=[pltpu.VMEM((MEMBERS, CHUNK + TAIL, 128), BF)],
        out_shape=jax.ShapeDtypeStruct((8, 8, CHUNK, 128), BF),
        name="analyse",
        compiler_params=pltpu.CompilerParams(vmem_limit_bytes=32 * 2**20),
    )(core, kept, other, var)


def finish_body(data, out):
    for j in range(4):
        for c in range(8):
            high, quarter = divmod(c, 4)
            out[j, high * CHUNK : (high + 1) * CHUNK, quarter * 128 : (quarter + 1) * 128] = data[
                c, j
            ].astype(F32)


def finish(data):
    return pl.pallas_call(
        finish_body,
        grid=(2,),
        in_specs=[pl.BlockSpec((8, 4, CHUNK, 128), lambda j: (0, j, 0, 0))],
        out_specs=pl.BlockSpec((4, VOX, STATE), lambda j: (j, 0, 0)),
        out_shape=jax.ShapeDtypeStruct((8, VOX, STATE), F32),
        name="finish",
        compiler_params=SMALL,
    )(data)


def pair(ring, low, core):
    return (2 * ring + low + core) % DEPTH


GROUPS = [
    [
        (pair(ring, low, core) * WIDTH + y) * CORES + core
        for low in range(2)
        for y in range(WIDTH)
    ]
    for core in range(CORES)
    for ring in range(RING)
]
WIDE_GROUPS = [
    [
        ((pair(ring, low, core) * WIDTH + y) * LENGTH + x) * CORES + core
        for low in range(2)
        for y in range(WIDTH)
        for x in range(LENGTH)
    ]
    for core in range(CORES)
    for ring in range(RING)
]


def swap(value, axes, groups=None):
    return lax.all_to_all(
        value, axes, split_axis=0, concat_axis=0, tiled=True, axis_index_groups=groups
    )


def trade(value):
    return swap(value, ("z", "y", "core"), GROUPS)


def per_device(
    state,
    noise,
    w_local,
    conn_weight,
    conn_index,
    boundary,
    send_pos,
    readout,
    observed,
    obs_value,
    obs_var,
    obs_pert,
):
    core = lax.axis_index("core")
    here = jnp.remainder(lax.axis_index("z") - core, DEPTH) // 2
    slab = prep(
        state, noise, conn_weight, conn_index, boundary, observed, obs_value, obs_var, obs_pert
    )
    slab = trade(slab)
    first, *packed = pack(state, noise, boundary)
    edge_rate = slab[:, VOX + AUX : VOX + AUX + BND, :].reshape(ROWS, STATE)
    sends = jnp.concatenate(
        [
            lax.dynamic_slice_in_dim(send_pos, pair(here, low, core) * WIDTH, WIDTH, 1)
            for low in range(2)
        ],
        axis=1,
    )
    source = jnp.arange(RING * PARTS, dtype=jnp.int32)
    level = jnp.remainder(source // WIDTH - core, DEPTH)
    base = jnp.remainder(here - level // 2, RING) * ROWS
    base = base + ((level % 2) * WIDTH + source % WIDTH) * BND
    colmap = jnp.transpose(base[:, None, None] + sends, (1, 0, 2)).reshape(PARTS, 1, HALO)
    own, halo, pick, ahead, begin = tables(slab, colmap)
    first = trade(first)
    kicks = {0: (first, ("rows", 0))}
    for steps, array in zip(BATCHES, packed):
        array = trade(array)
        for place, t in enumerate(steps):
            kicks[t] = (array, ("batch", place))
    edge_current = current = None
    rate = slab
    for t in range(STEPS):
        table = [edge_rate]
        for o in range(1, RING):
            table.append(
                lax.ppermute(edge_rate, "z", [(i, (i + 2 * o) % DEPTH) for i in range(DEPTH)])
            )
        kick, place = kicks[t]
        if t < STEPS - 1:
            if t == 0:
                found, row = slab, ("rows", (VOX + AUX) // BND + 1)
            elif t == 1:
                found, row = first, ("rows", VOX // BND)
            else:
                found, row = kicks[t - 1]
            edge_rate, edge_current = edge(begin, ahead, w_local, found, row, table, edge_current)
            current, rate, begin = step(
                t in ROOMY, rate, own, halo, pick, w_local, kick, place, current, table
            )
        else:
            chunks = last(
                rate, own, halo, w_local, kick, place, current, table, slab, readout[None, :]
            )
    wide = chunks.reshape(PARTS * LENGTH, CORES, CHUNK + TAIL, 128)
    wide = swap(wide, ("z", "y", "x", "core"), WIDE_GROUPS)
    kept = lax.dynamic_index_in_dim(wide, core, 1, keepdims=False)
    other = lax.dynamic_index_in_dim(wide, 1 - core, 1, keepdims=False)
    other = lax.ppermute(other, "core", [(0, 1), (1, 0)])
    result = swap(analyse(core.reshape(1), kept, other, obs_var), ("x", "core"))
    return finish(result)


def solution(mesh):
    fine = Mesh(
        mesh.devices.reshape(DEPTH, WIDTH, LENGTH, CORES), ("z", "y", "x", "core")
    )
    dom, member = ("z", "y"), ("x", "core")
    in_specs = (
        P(member, dom, None),
        P(None, member, dom, None),
        P(),
        P(None, dom),
        P(None, dom),
        P(dom, None),
        P(),
        P(),
        P(dom, None),
        P(dom, None),
        P(dom, None),
        P(member, dom, None),
    )
    return jax.shard_map(
        per_device, mesh=fine, in_specs=in_specs, out_specs=P(member, dom, None), check_vma=False
    )
```

```python
import functools

import jax
import jax.numpy as jnp
from jax import lax
from jax.experimental import pallas as pl
from jax.experimental.pallas import tpu as pltpu
from jax.sharding import Mesh, PartitionSpec as P

STATE = 512
VOX = 96
STEPS = 8
BND = 8
OBS = 64
KIN = 16
HALO = 128
PARTS = 8
RING = 4
DEPTH, WIDTH, LENGTH, CORES = 8, 4, 4, 2
ROWS = PARTS * BND
AUX = 16
TAIL = 8
CHUNK = 48
MEMBERS = 64
BF = jnp.bfloat16
F32 = jnp.float32
HIGH = lax.Precision.HIGHEST


def iota(shape, axis):
    return lax.broadcasted_iota(jnp.int32, shape, axis)


def dot(a, b):
    return jnp.dot(a, b, preferred_element_type=F32)


def pieces(value):
    high = value.astype(BF).astype(F32)
    rest = value - high
    middle = rest.astype(BF).astype(F32)
    return high, middle, rest - middle


def stack_rows(rows, shape):
    row = iota(shape, 0)
    total = jnp.zeros(shape, F32)
    for place, value in enumerate(rows):
        total = jnp.where(row == place, jnp.broadcast_to(value, shape), total)
    return total


def chosen_rows(bound):
    eye = iota((AUX, BND), 0) == iota((AUX, BND), 1)
    column = jnp.sum(jnp.where(eye, bound.astype(F32), 0.0), axis=1, keepdims=True)
    shape = (AUX, 128)
    match = (iota(shape, 1).astype(F32) == column) & (iota(shape, 0) < BND)
    return jnp.where(match, 1.0, 0.0).astype(BF)


def prep_body(state, noise, weight, index, bound, observed, value, var, pert, slab):
    chosen = chosen_rows(bound[...])
    for j in range(4):
        rate = jnp.tanh(state[j]).astype(BF)
        slab[j, 0:VOX, :] = rate
        slab[j, VOX : VOX + AUX, :] = jnp.zeros((AUX, STATE), BF)
        slab[j, VOX : VOX + AUX, 0:VOX] = weight[...].astype(BF)
        slab[j, VOX : VOX + AUX, 128 : 128 + VOX] = index[...].astype(F32).astype(BF)
        shifted = value[...] + jnp.sqrt(var[...]) * pert[j]
        info = (observed[...].astype(F32),) + pieces(shifted)
        slab[j, VOX : VOX + AUX, 256 : 256 + OBS] = stack_rows(info, (AUX, OBS)).astype(BF)
        slab[j, VOX : VOX + AUX, 384:512] = chosen
        start = (0.5 * state[j] + noise[0, j].astype(F32)).astype(BF)
        pick = chosen[:, 0:VOX]
        both = (dot(pick, rate)[0:BND], dot(pick, start)[0:BND])
        slab[j, VOX + AUX : VOX + 2 * AUX, :] = jnp.concatenate(both, axis=0).astype(BF)


ROOMY = tuple(range(8))
SMALL = pltpu.CompilerParams(vmem_limit_bytes=20 * 2**20)


def whole(*shape):
    return pl.BlockSpec(shape, lambda q: (0,) * len(shape))


def prep(state, noise, weight, index, bound, observed, value, var, pert):
    return pl.pallas_call(
        prep_body,
        grid=(PARTS // 4,),
        in_specs=[
            pl.BlockSpec((4, VOX, STATE), lambda j: (j, 0, 0)),
            pl.BlockSpec((1, 4, VOX, STATE), lambda j: (0, j, 0, 0)),
            whole(KIN, VOX),
            whole(KIN, VOX),
            whole(1, BND),
            whole(1, OBS),
            whole(1, OBS),
            whole(1, OBS),
            pl.BlockSpec((4, 1, OBS), lambda j: (j, 0, 0)),
        ],
        out_specs=pl.BlockSpec((4, VOX + 2 * AUX, STATE), lambda j: (j, 0, 0)),
        out_shape=jax.ShapeDtypeStruct((PARTS, VOX + 2 * AUX, STATE), BF),
        name="prep",
    )(state, noise, weight, index, bound, observed, value, var, pert)


def pack_body(state, noise, bound, first, *packed):
    chosen = chosen_rows(bound[...])[:, 0:VOX]
    start = (0.5 * state[0] + noise[0, 0].astype(F32)).astype(BF)
    first[0, 0:VOX, :] = start
    found = [dot(chosen, noise[t, 0])[0:BND].astype(BF) for t in range(1, STEPS)]
    found.append(jnp.zeros((BND, STATE), BF))
    first[0, VOX:, :] = found[0]
    for steps, out in zip(BATCHES, packed):
        for place, t in enumerate(steps):
            out[0, place, 0:VOX, :] = noise[t, 0]
            out[0, place, VOX:, :] = found[t]


BATCHES = ((1,), (2,), (3,), (4,), (5,), (6, 7))
FIRST = VOX + BND


def pack(state, noise, bound):
    sizes = [len(steps) for steps in BATCHES]
    return pl.pallas_call(
        pack_body,
        grid=(PARTS,),
        in_specs=[
            pl.BlockSpec((1, VOX, STATE), lambda j: (j, 0, 0)),
            pl.BlockSpec((STEPS, 1, VOX, STATE), lambda j: (0, j, 0, 0)),
            whole(1, BND),
        ],
        out_specs=[pl.BlockSpec((1, FIRST, STATE), lambda j: (j, 0, 0))]
        + [pl.BlockSpec((1, n, FIRST, STATE), lambda j: (j, 0, 0, 0)) for n in sizes],
        out_shape=[jax.ShapeDtypeStruct((PARTS, FIRST, STATE), BF)]
        + [jax.ShapeDtypeStruct((PARTS, n, FIRST, STATE), BF) for n in sizes],
        name="pack",
        cost_estimate=pl.CostEstimate(flops=10**9, bytes_accessed=14 * 10**6, transcendentals=0),
    )(state, noise, bound)


def tables_body(slab, colmap, own, halo, pick, ahead, start):
    weight = slab[0, VOX : VOX + AUX, 0:128].astype(F32)
    index = slab[0, VOX : VOX + AUX, 128:256].astype(F32)
    row = iota((256, 128), 0).astype(F32)
    spread = jnp.zeros((256, 128), F32)
    for k in range(KIN):
        spread = spread + jnp.where(row == index[k : k + 1, :], weight[k : k + 1, :], 0.0)
    local = jnp.transpose(spread[0:128, :])[0:VOX, :]
    slots = jnp.transpose(spread[VOX : VOX + HALO, :])[0:VOX, :].astype(BF)
    place = (iota((RING * ROWS, HALO), 0) == colmap[0]).astype(F32).astype(BF)
    far = lax.dot_general(slots, place, (((1,), (1,)), ((), ())), preferred_element_type=F32).astype(BF)
    chosen = slab[0, VOX : VOX + AUX, 384:512][:, 0:VOX]
    own_matrix = local[:, 0:VOX].astype(BF)
    own[0] = own_matrix
    halo[0] = far
    chosen_own = dot(chosen, own_matrix)
    both = jnp.concatenate([chosen.astype(F32)[0:BND], chosen_own[0:BND]], axis=0).astype(BF)
    pick[0] = both
    ahead[...] = dot(chosen, far)[0:BND].astype(BF)
    found = dot(both, slab[0, 0:VOX, :])
    start[...] = found[0:BND] + found[BND : 2 * BND]


def tables(slab, colmap):
    return pl.pallas_call(
        tables_body,
        grid=(PARTS,),
        in_specs=[
            pl.BlockSpec((1, VOX + AUX, STATE), lambda q: (q, 0, 0)),
            pl.BlockSpec((1, 1, HALO), lambda q: (q, 0, 0)),
        ],
        out_specs=[
            pl.BlockSpec((1, VOX, VOX), lambda q: (q, 0, 0)),
            pl.BlockSpec((1, VOX, RING * ROWS), lambda q: (q, 0, 0)),
            pl.BlockSpec((1, 2 * BND, VOX), lambda q: (q, 0, 0)),
            pl.BlockSpec((BND, RING * ROWS), lambda q: (q, 0)),
            pl.BlockSpec((BND, STATE), lambda q: (q, 0)),
        ],
        out_shape=[
            jax.ShapeDtypeStruct((PARTS, VOX, VOX), BF),
            jax.ShapeDtypeStruct((PARTS, VOX, RING * ROWS), BF),
            jax.ShapeDtypeStruct((PARTS, 2 * BND, VOX), BF),
            jax.ShapeDtypeStruct((ROWS, RING * ROWS), BF),
            jax.ShapeDtypeStruct((ROWS, STATE), F32),
        ],
        name="tables",
        compiler_params=SMALL,
        cost_estimate=pl.CostEstimate(flops=10**9, bytes_accessed=10**7, transcendentals=0),
    )(slab, colmap)


def edge_body(begin, ahead, w, noise, r0, r1, r2, r3, *refs):
    current, (rate_out, current_out) = refs[:-2], refs[-2:]
    table = jnp.concatenate([r0[...], r1[...], r2[...], r3[...]], axis=0)
    inputs = (begin[...] + dot(ahead[...], table)).astype(BF)
    value = 0.5 * dot(inputs, w[...]) + noise[...].astype(F32).reshape(ROWS, STATE)
    if current:
        value = value + 0.5 * current[0][...]
    current_out[...] = value
    rate_out[...] = jnp.tanh(value).astype(BF)


def edge(begin, ahead, w, noise, place, table, current):
    more = [] if current is None else [current]
    kind, place = place
    if kind == "rows":
        early = pl.BlockSpec((PARTS, BND, STATE), lambda q: (0, place, 0))
    else:
        early = pl.BlockSpec((PARTS, 1, BND, STATE), lambda q: (0, place, VOX // BND, 0))
    return pl.pallas_call(
        edge_body,
        grid=(1,),
        in_specs=[
            whole(ROWS, STATE),
            whole(ROWS, RING * ROWS),
            whole(STATE, STATE),
            early,
        ]
        + [whole(ROWS, STATE)] * (RING + len(more)),
        out_specs=[whole(ROWS, STATE), whole(ROWS, STATE)],
        out_shape=[
            jax.ShapeDtypeStruct((ROWS, STATE), BF),
            jax.ShapeDtypeStruct((ROWS, STATE), F32),
        ],
        name="edge",
        compiler_params=SMALL,
        cost_estimate=pl.CostEstimate(flops=10**8, bytes_accessed=10**6, transcendentals=0),
    )(begin, ahead, w, noise, *table, *more)


GROUP = 4


def advance(rate, own, halo, w, noise, current, table):
    mine = jnp.concatenate([dot(own[i], rate[i]) for i in range(GROUP)], axis=0)
    matrix = jnp.concatenate([halo[i] for i in range(GROUP)], axis=0)
    far = dot(matrix, jnp.concatenate([r[...] for r in table], axis=0))
    inputs = rate[...].astype(F32).reshape(GROUP * VOX, STATE) + mine + far
    mixed = dot(inputs.astype(BF), w[...])
    value = 0.5 * mixed + noise[...].astype(F32).reshape(GROUP * VOX, STATE)
    if current is not None:
        value = value + 0.5 * current[...].reshape(GROUP * VOX, STATE)
    return value


def step_body(has_current, *refs):
    rate, own, halo, pick, w, noise = refs[:6]
    refs = refs[6:]
    current = None
    if has_current:
        current, refs = refs[0], refs[1:]
    table, (current_out, rate_out, begin_out) = refs[:RING], refs[RING:]
    value = advance(rate, own, halo, w, noise, current, table)
    fresh = jnp.tanh(value).astype(BF)
    current_out[...] = value.reshape(GROUP, VOX, STATE)
    rate_out[...] = fresh.reshape(GROUP, VOX, STATE)
    for i in range(GROUP):
        found = dot(pick[i], fresh[i * VOX : (i + 1) * VOX])
        begin_out[i * BND : (i + 1) * BND, :] = found[0:BND] + found[BND : 2 * BND]


def common_specs(has_current, with_pick, place):
    part = lambda *shape: pl.BlockSpec((GROUP,) + shape, lambda q: (q, 0, 0))
    kind, place = place
    if kind == "rows":
        kick = pl.BlockSpec((GROUP, VOX, STATE), lambda q: (q, place, 0))
    else:
        kick = pl.BlockSpec((GROUP, 1, VOX, STATE), lambda q: (q, place, 0, 0))
    specs = [part(VOX, STATE), part(VOX, VOX), part(VOX, RING * ROWS)]
    if with_pick:
        specs.append(part(2 * BND, VOX))
    specs += [whole(STATE, STATE), kick]
    if has_current:
        specs.append(part(VOX, STATE))
    specs += [whole(ROWS, STATE)] * RING
    return specs


STEP_COST = pl.CostEstimate(flops=2 * 10**9, bytes_accessed=6 * 10**6, transcendentals=4 * 10**5)


def step(roomy, rate, own, halo, pick, w, noise, place, current, table):
    args = [rate, own, halo, pick, w, noise] + ([] if current is None else [current]) + list(table)
    return pl.pallas_call(
        functools.partial(step_body, current is not None),
        grid=(PARTS // GROUP,),
        in_specs=common_specs(current is not None, True, place),
        out_specs=[
            pl.BlockSpec((GROUP, VOX, STATE), lambda q: (q, 0, 0)),
            pl.BlockSpec((GROUP, VOX, STATE), lambda q: (q, 0, 0)),
            pl.BlockSpec((GROUP * BND, STATE), lambda q: (q, 0)),
        ],
        out_shape=[
            jax.ShapeDtypeStruct((PARTS, VOX, STATE), F32),
            jax.ShapeDtypeStruct((PARTS, VOX, STATE), BF),
            jax.ShapeDtypeStruct((ROWS, STATE), F32),
        ],
        name="step",
        compiler_params=None if roomy else SMALL,
        cost_estimate=STEP_COST,
    )(*args)


def last_body(rate, own, halo, w, noise, current, r0, r1, r2, r3, extra, readout, out):
    value = advance(rate, own, halo, w, noise, current, (r0, r1, r2, r3))
    weighted = value * readout[...]
    for i in range(GROUP):
        image_rows = jnp.sum(weighted[i * VOX : (i + 1) * VOX], axis=1, keepdims=True)
        info = extra[i].astype(F32)
        observed = info[0:1, 0:OBS]
        shifted = info[1:2, 0:OBS] + info[2:3, 0:OBS] + info[3:4, 0:OBS]
        seen = iota((VOX, OBS), 0).astype(F32) == observed
        image = jnp.sum(jnp.where(seen, image_rows, 0.0), axis=0, keepdims=True)
        image_block = stack_rows(pieces(image), (TAIL, OBS)).astype(BF)
        innov_block = stack_rows(pieces(shifted - image), (TAIL, OBS)).astype(BF)
        for c in range(8):
            high, quarter = divmod(c, 4)
            begin = i * VOX + high * CHUNK
            out[i * 8 + c, 0:CHUNK, :] = value[
                begin : begin + CHUNK, quarter * 128 : (quarter + 1) * 128
            ].astype(BF)
            out[i * 8 + c, CHUNK : CHUNK + TAIL, 0:OBS] = image_block
            out[i * 8 + c, CHUNK : CHUNK + TAIL, OBS : 2 * OBS] = innov_block


def last(rate, own, halo, w, noise, place, current, table, slab, readout):
    return pl.pallas_call(
        last_body,
        grid=(PARTS // GROUP,),
        in_specs=common_specs(True, False, place)
        + [
            pl.BlockSpec((GROUP, AUX, 128), lambda q: (q, VOX // AUX, 2)),
            pl.BlockSpec((1, STATE), lambda q: (0, 0)),
        ],
        out_specs=pl.BlockSpec((GROUP * 8, CHUNK + TAIL, 128), lambda q: (q, 0, 0)),
        out_shape=jax.ShapeDtypeStruct((PARTS * 8, CHUNK + TAIL, 128), BF),
        name="last",
        cost_estimate=STEP_COST,
    )(rate, own, halo, w, noise, current, *table, slab, readout)


def analyse_body(core, kept, other, var, out, data):
    half = MEMBERS // 2
    is_first = core[0] == 0
    data[0:half] = jnp.where(is_first, kept[...], other[...])
    data[half:] = jnp.where(is_first, other[...], kept[...])
    extra = data[:, CHUNK : CHUNK + TAIL, :].astype(F32)
    both = jnp.sum(extra, axis=1)
    image, innov = both[:, 0:OBS], both[:, OBS : 2 * OBS]
    anomaly = image - jnp.mean(image, axis=0, keepdims=True)
    flipped = jnp.transpose(anomaly)
    covar = jnp.dot(flipped, anomaly, precision=HIGH, preferred_element_type=F32) / (MEMBERS - 1)
    square = (OBS, OBS)
    covar = covar + jnp.where(iota(square, 0) == iota(square, 1), var[...], 0.0)
    work = jnp.concatenate([covar, flipped], axis=1)
    row = iota((OBS, 2 * OBS), 0)
    for k in range(OBS):
        pivot = work[k : k + 1, :] / work[k : k + 1, k : k + 1]
        work = jnp.where(row == k, pivot, work - work[:, k : k + 1] * pivot)
    solved = work[:, OBS : 2 * OBS]
    mixing = jnp.dot(innov, solved, precision=HIGH, preferred_element_type=F32) / (MEMBERS - 1)
    mixing = mixing - jnp.mean(mixing, axis=1, keepdims=True)
    wide = MEMBERS * 16
    repeat = jnp.where(
        lax.shift_right_logical(iota((wide, MEMBERS), 0), 4) == iota((wide, MEMBERS), 1), 1.0, 0.0
    ).astype(BF)
    tall = dot(repeat, mixing.astype(BF)).astype(BF)
    large = lax.dot_general(tall, repeat, (((1,), (1,)), ((), ())), preferred_element_type=F32)
    same = (iota((wide, wide), 0) & 15) == (iota((wide, wide), 1) & 15)
    large = jnp.where(same, large, 0.0).astype(BF)
    for b in range(CHUNK // 16):
        rows = data[:, b * 16 : (b + 1) * 16, :].reshape(wide, 128)
        result = (rows.astype(F32) + dot(large, rows)).astype(BF).reshape(MEMBERS, 16, 128)
        for m in range(MEMBERS):
            owner = (m % LENGTH) * CORES + m // half
            out[owner, m % half // LENGTH, b * 16 : (b + 1) * 16, :] = result[m]


def analyse(core, kept, other, var):
    vmem = pl.BlockSpec(memory_space=pltpu.VMEM)
    return pl.pallas_call(
        analyse_body,
        in_specs=[pl.BlockSpec(memory_space=pltpu.SMEM), vmem, vmem, vmem],
        out_specs=vmem,
        scratch_shapes=[pltpu.VMEM((MEMBERS, CHUNK + TAIL, 128), BF)],
        out_shape=jax.ShapeDtypeStruct((8, 8, CHUNK, 128), BF),
        name="analyse",
        compiler_params=pltpu.CompilerParams(vmem_limit_bytes=32 * 2**20),
    )(core, kept, other, var)


def finish_body(data, out):
    for j in range(4):
        for c in range(8):
            high, quarter = divmod(c, 4)
            out[j, high * CHUNK : (high + 1) * CHUNK, quarter * 128 : (quarter + 1) * 128] = data[
                c, j
            ].astype(F32)


def finish(data):
    return pl.pallas_call(
        finish_body,
        grid=(2,),
        in_specs=[pl.BlockSpec((8, 4, CHUNK, 128), lambda j: (0, j, 0, 0))],
        out_specs=pl.BlockSpec((4, VOX, STATE), lambda j: (j, 0, 0)),
        out_shape=jax.ShapeDtypeStruct((8, VOX, STATE), F32),
        name="finish",
        compiler_params=SMALL,
    )(data)


def pair(ring, low, core):
    return (2 * ring + low + core) % DEPTH


GROUPS = [
    [
        (pair(ring, low, core) * WIDTH + y) * CORES + core
        for low in range(2)
        for y in range(WIDTH)
    ]
    for core in range(CORES)
    for ring in range(RING)
]
WIDE_GROUPS = [
    [
        ((pair(ring, low, core) * WIDTH + y) * LENGTH + x) * CORES + core
        for low in range(2)
        for y in range(WIDTH)
        for x in range(LENGTH)
    ]
    for core in range(CORES)
    for ring in range(RING)
]


def swap(value, axes, groups=None):
    return lax.all_to_all(
        value, axes, split_axis=0, concat_axis=0, tiled=True, axis_index_groups=groups
    )


def trade(value):
    return swap(value, ("z", "y", "core"), GROUPS)


def per_device(
    state,
    noise,
    w_local,
    conn_weight,
    conn_index,
    boundary,
    send_pos,
    readout,
    observed,
    obs_value,
    obs_var,
    obs_pert,
):
    core = lax.axis_index("core")
    here = jnp.remainder(lax.axis_index("z") - core, DEPTH) // 2
    slab = prep(
        state, noise, conn_weight, conn_index, boundary, observed, obs_value, obs_var, obs_pert
    )
    slab = trade(slab)
    first, *packed = pack(state, noise, boundary)
    edge_rate = slab[:, VOX + AUX : VOX + AUX + BND, :].reshape(ROWS, STATE)
    sends = jnp.concatenate(
        [
            lax.dynamic_slice_in_dim(send_pos, pair(here, low, core) * WIDTH, WIDTH, 1)
            for low in range(2)
        ],
        axis=1,
    )
    source = jnp.arange(RING * PARTS, dtype=jnp.int32)
    level = jnp.remainder(source // WIDTH - core, DEPTH)
    base = jnp.remainder(here - level // 2, RING) * ROWS
    base = base + ((level % 2) * WIDTH + source % WIDTH) * BND
    colmap = jnp.transpose(base[:, None, None] + sends, (1, 0, 2)).reshape(PARTS, 1, HALO)
    own, halo, pick, ahead, begin = tables(slab, colmap)
    first = trade(first)
    kicks = {0: (first, ("rows", 0))}
    for steps, array in zip(BATCHES, packed):
        array = trade(array)
        for place, t in enumerate(steps):
            kicks[t] = (array, ("batch", place))
    edge_current = current = None
    rate = slab
    for t in range(STEPS):
        table = [edge_rate]
        for o in range(1, RING):
            table.append(
                lax.ppermute(edge_rate, "z", [(i, (i + 2 * o) % DEPTH) for i in range(DEPTH)])
            )
        kick, place = kicks[t]
        if t < STEPS - 1:
            if t == 0:
                found, row = slab, ("rows", (VOX + AUX) // BND + 1)
            elif t == 1:
                found, row = first, ("rows", VOX // BND)
            else:
                found, row = kicks[t - 1]
            edge_rate, edge_current = edge(begin, ahead, w_local, found, row, table, edge_current)
            current, rate, begin = step(
                t in ROOMY, rate, own, halo, pick, w_local, kick, place, current, table
            )
        else:
            chunks = last(
                rate, own, halo, w_local, kick, place, current, table, slab, readout[None, :]
            )
    wide = chunks.reshape(PARTS * LENGTH, CORES, CHUNK + TAIL, 128)
    wide = swap(wide, ("z", "y", "x", "core"), WIDE_GROUPS)
    kept = lax.dynamic_index_in_dim(wide, core, 1, keepdims=False)
    other = lax.dynamic_index_in_dim(wide, 1 - core, 1, keepdims=False)
    other = lax.ppermute(other, "core", [(0, 1), (1, 0)])
    result = swap(analyse(core.reshape(1), kept, other, obs_var), ("x", "core"))
    return finish(result)


def solution(mesh):
    fine = Mesh(
        mesh.devices.reshape(DEPTH, WIDTH, LENGTH, CORES), ("z", "y", "x", "core")
    )
    dom, member = ("z", "y"), ("x", "core")
    in_specs = (
        P(member, dom, None),
        P(None, member, dom, None),
        P(),
        P(None, dom),
        P(None, dom),
        P(dom, None),
        P(),
        P(),
        P(dom, None),
        P(dom, None),
        P(dom, None),
        P(member, dom, None),
    )
    return jax.shard_map(
        per_device, mesh=fine, in_specs=in_specs, out_specs=P(member, dom, None), check_vma=False
    )
```
